32 devices in a mesh: dom: 4 (over z), shard: 8 (over y, x, core).
Axes of the slice: x: 2, y: 2, z: 4, core: 2. Of those that a mesh axis runs over, the one named last changes fastest.
Arguments:
- features: bfloat16 [131072, 1024], P(('dom', 'shard')), may hold values from -6 to 6
- enc_weight: bfloat16 [1024, 512], replicated, may hold values from -0.1875 to 0.1875
- pack_index: int32 [4, 8, 8, 512], P('dom', 'shard'), may hold values from 0 to 4095, as said below
- place_index: int32 [4, 8, 4096], P('dom', 'shard'), may hold values from 0 to 4095, as said below
- halo_send_one: int32 [4, 8, 4, 8, 16], P('dom', 'shard'), may hold values from 0 to 4096, as said below
- halo_send_two: int32 [4, 8, 4, 8, 16], P('dom', 'shard'), may hold values from 0 to 4096, as said below
- tile_index_one: int32 [1024, 6], P(('dom', 'shard')), may hold values from 0 to 35
- tile_index_two: int32 [1024, 6], P(('dom', 'shard')), may hold values from 0 to 35
- tile_live_one: int32 [1024], P(('dom', 'shard')), may hold values from 1 to 6, as said below
- tile_live_two: int32 [1024], P(('dom', 'shard')), may hold values from 1 to 6, as said below
- tiles_one: bfloat16 [1024, 6, 128, 128], P(('dom', 'shard')), may hold values from 0 to 2, as said below
- tiles_two: bfloat16 [1024, 6, 128, 128], P(('dom', 'shard')), may hold values from 0 to 2, as said below
- degree: int32 [131072], P(('dom', 'shard')), may hold values from 32 to 255
- self_weight_one: bfloat16 [512, 512], replicated, may hold values from -0.25 to 0.25
- neigh_weight_one: bfloat16 [512, 512], replicated, may hold values from -0.25 to 0.25
- self_weight_two: bfloat16 [512, 512], replicated, may hold values from -0.25 to 0.25
- neigh_weight_two: bfloat16 [512, 512], replicated, may hold values from -0.25 to 0.25
- head_weight: bfloat16 [512], replicated, may hold values from -0.25 to 0.25
Outputs:
- embedding: bfloat16 [131072, 512], P(('dom', 'shard'))
- probability: float32 [131072], P(('dom', 'shard'))
The draws below stay inside these ranges and needn't reach their ends.
Inputs may be any that keep to these rules, and one draw needn't show every extreme that they name: pack_index[d, s, t, :] lists the 512 hash-order rows that device s of group d sends to owner t; every local row is sent exactly once. place_index[d, t, :] is a permutation of the slots that owner t receives. halo_send_one[d, s, d2, s2, :] lists rows of device (d, s) for device (d2, s2), then 4096 in empty slots; a device sends nothing to itself, exactly 16 rows to one device and 1 to 16 rows to every other. `halo_send_two`: as halo_send_one. `tile_live_one`: every device has a block with all 6 slots live. `tile_live_two`: every device has a block with all 6 slots live. `tiles_one`: nonnegative edge weights. `tiles_two`: nonnegative edge weights.
All inputs are finite; a program needn't handle non-finite values.
Results may differ from the reference program's by a relative error of at most 0.0054.
Values may be sent and summed in bfloat16 or wider, within the bound.
A program may use at most 192 MiB of HBM per device.

```python
import jax
import jax.numpy as jnp
from jax import lax

IN_WIDTH = 1024
WIDTH = 512
ROWS_DEV = 4096
TILE_SIZE = 128
TILE_SLOTS = 6
BOUNDARY_CAP = 16
GROUPS = 4
GROUP_SIZE = 8
DEVICE_COUNT = 32
TARGETS = 131072
BLOCKS_DEV = 32
BLOCKS_ALL = 1024
SOURCE_BLOCKS = 36
RELAY_CAP = 512
N_DOM = 4
N_SHARD = 8


def relay_tables(key):

    def one_group(group_key):
        key_order, key_place = jax.random.split(group_key)
        orders = jax.vmap(lambda kk: jax.random.permutation(kk, ROWS_DEV))(jax.random.split(key_order, GROUP_SIZE))
        packing = orders.reshape(GROUP_SIZE, GROUP_SIZE, RELAY_CAP).astype(jnp.int32)
        placing = jax.vmap(lambda kk: jax.random.permutation(kk, ROWS_DEV))(jax.random.split(key_place, GROUP_SIZE)).astype(jnp.int32)
        return (packing, placing)
    return jax.vmap(one_group)(jax.random.split(jax.random.fold_in(key, 11), GROUPS))


def draw_pack_index(key, part):
    return relay_tables(key)[0]


def draw_place_index(key, part):
    return relay_tables(key)[1]


def halo_table(key):
    key_count, key_rows = jax.random.split(key)
    counts = jax.random.randint(key_count, (DEVICE_COUNT, DEVICE_COUNT), 1, BOUNDARY_CAP + 1)
    source = jnp.arange(DEVICE_COUNT)[:, None]
    target = jnp.arange(DEVICE_COUNT)[None, :]
    counts = jnp.where(target == (source + DEVICE_COUNT // 2 + 1) % DEVICE_COUNT, BOUNDARY_CAP, counts)
    counts = jnp.where(target == source, 0, counts)
    picks = jax.random.randint(key_rows, (DEVICE_COUNT, DEVICE_COUNT, BOUNDARY_CAP), 0, ROWS_DEV)
    slots = jnp.arange(BOUNDARY_CAP)
    table = jnp.where(slots[None, None, :] < counts[:, :, None], picks, ROWS_DEV)
    return table.reshape(GROUPS, GROUP_SIZE, GROUPS, GROUP_SIZE, BOUNDARY_CAP).astype(jnp.int32)


def draw_halo_send_one(key, part):
    return halo_table(jax.random.fold_in(key, 21))


def draw_halo_send_two(key, part):
    return halo_table(jax.random.fold_in(key, 22))


def live_table(key):
    key_count, key_full = jax.random.split(key)
    counts = jax.random.randint(key_count, (DEVICE_COUNT, BLOCKS_DEV), 1, TILE_SLOTS + 1)
    full = jax.random.randint(key_full, (DEVICE_COUNT,), 0, BLOCKS_DEV)
    counts = jnp.where(jnp.arange(BLOCKS_DEV)[None, :] == full[:, None], TILE_SLOTS, counts)
    return counts.reshape(BLOCKS_ALL).astype(jnp.int32)


def draw_tile_live_one(key, part):
    return live_table(jax.random.fold_in(key, 31))


def draw_tile_live_two(key, part):
    return live_table(jax.random.fold_in(key, 32))


def tile_table(key):
    key_mask, key_value = jax.random.split(key)
    shape = (BLOCKS_ALL, TILE_SLOTS, TILE_SIZE, TILE_SIZE)
    present = jax.random.bernoulli(key_mask, 0.5, shape).astype(jnp.float32)
    value = jax.random.uniform(key_value, shape, jnp.float32, 0.5, 1.5)
    return (present * value).astype(jnp.bfloat16)


def draw_tiles_one(key, part):
    return tile_table(jax.random.fold_in(key, 41))


def draw_tiles_two(key, part):
    return tile_table(jax.random.fold_in(key, 42))


def plant(array, rng, least, largest):
    longest = array.shape.index(max(array.shape))
    spots = []
    for shift in (0, 1):
        where = [jax.random.randint(jax.random.fold_in(rng, axis), (), 0, length) for axis, length in enumerate(array.shape)]
        where[longest] = (where[longest] + shift) % array.shape[longest]
        spots.append(tuple(where))
    return array.at[spots[0]].set(least).at[spots[1]].set(largest)


def levels(rng, extent, pieces, low, largest):
    gain, own = 1.0, jax.random.fold_in(rng, 6)
    for position, parts in pieces:
        heights = jnp.exp(jax.random.uniform(jax.random.fold_in(own, position), (parts,), jnp.float32, low / len(pieces), largest / len(pieces)))
        gain = gain * jnp.repeat(heights, extent[position] // parts).reshape([-1 if axis == position else 1 for axis in range(len(extent))])
    return gain


def centred(own_key, shape, deviation, reach, cuts=(), kind=jnp.bfloat16):
    entries = deviation * jax.random.normal(own_key, shape, jnp.float32)
    if cuts:
        entries = entries * levels(own_key, shape, cuts, -0.22, 0.18)
    return jnp.clip(entries, -reach, reach).astype(kind)


def setup_inputs(seed: int = 0) -> dict:
    streams_of = jax.random.split(jax.random.key(seed), 19)
    features = centred(streams_of[0], (TARGETS, IN_WIDTH), 1.0, 6.0, ((0, 32),))
    enc_weight = centred(streams_of[1], (IN_WIDTH, WIDTH), IN_WIDTH ** -0.5, 0.1875)
    pack_index = draw_pack_index(jax.random.fold_in(streams_of[18], 71), 0)
    place_index = draw_place_index(jax.random.fold_in(streams_of[18], 71), 0)
    halo_send_one = draw_halo_send_one(jax.random.fold_in(streams_of[18], 71), 0)
    halo_send_two = draw_halo_send_two(jax.random.fold_in(streams_of[18], 71), 0)
    tile_index_one = plant(jax.random.randint(streams_of[6], (BLOCKS_ALL, TILE_SLOTS), 0, SOURCE_BLOCKS), jax.random.fold_in(streams_of[6], 1), 0, SOURCE_BLOCKS - 1).astype(jnp.int32)
    tile_index_two = plant(jax.random.randint(streams_of[7], (BLOCKS_ALL, TILE_SLOTS), 0, SOURCE_BLOCKS), jax.random.fold_in(streams_of[7], 1), 0, SOURCE_BLOCKS - 1).astype(jnp.int32)
    tile_live_one = draw_tile_live_one(jax.random.fold_in(streams_of[18], 71), 0)
    tile_live_two = draw_tile_live_two(jax.random.fold_in(streams_of[18], 71), 0)
    tiles_one = draw_tiles_one(jax.random.fold_in(streams_of[18], 71), 0)
    tiles_two = draw_tiles_two(jax.random.fold_in(streams_of[18], 71), 0)
    degree = plant(jax.random.randint(streams_of[12], (TARGETS,), 32, 256), jax.random.fold_in(streams_of[12], 1), 32, 255).astype(jnp.int32)
    self_weight_one = centred(streams_of[13], (WIDTH, WIDTH), WIDTH ** -0.5, 0.25)
    neigh_weight_one = centred(streams_of[14], (WIDTH, WIDTH), WIDTH ** -0.5, 0.25)
    self_weight_two = centred(streams_of[15], (WIDTH, WIDTH), WIDTH ** -0.5, 0.25)
    neigh_weight_two = centred(streams_of[16], (WIDTH, WIDTH), WIDTH ** -0.5, 0.25)
    head_weight = centred(streams_of[17], (WIDTH,), WIDTH ** -0.5, 0.25)
    return {"features": features, "enc_weight": enc_weight, "pack_index": pack_index, "place_index": place_index, "halo_send_one": halo_send_one, "halo_send_two": halo_send_two, "tile_index_one": tile_index_one, "tile_index_two": tile_index_two, "tile_live_one": tile_live_one, "tile_live_two": tile_live_two, "tiles_one": tiles_one, "tiles_two": tiles_two, "degree": degree, "self_weight_one": self_weight_one, "neigh_weight_one": neigh_weight_one, "self_weight_two": self_weight_two, "neigh_weight_two": neigh_weight_two, "head_weight": head_weight}


def sage_layer(hidden_in, halo_send, tile_index, tile_live, tiles, degree, self_weight, neigh_weight):
    count = N_DOM * N_SHARD
    width = hidden_in.shape[-1]
    padded = jnp.concatenate([hidden_in, jnp.zeros((count, 1, width), jnp.bfloat16)], axis=1)
    sendlist = halo_send.reshape(count, count, BOUNDARY_CAP)

    def per_device(packed):
        device, own_rows, index_dev, live_dev, tiles_dev, degree_dev = packed
        columns = lax.dynamic_index_in_dim(sendlist, device, axis=1, keepdims=False)
        boundary = jax.vmap(lambda table, picks: table[picks])(padded, columns).reshape(count * BOUNDARY_CAP, width)
        sources = jnp.concatenate([own_rows, boundary], axis=0).reshape(-1, TILE_SIZE, width)
        slot_live = jnp.arange(TILE_SLOTS, dtype=jnp.int32)[None, :] < live_dev[:, None]
        masked = jnp.where(slot_live[:, :, None, None], tiles_dev, jnp.zeros((), jnp.bfloat16))
        picked = sources[index_dev]
        summed = jnp.einsum('bkij,bkjf->bif', masked.astype(jnp.float32), picked.astype(jnp.float32)).reshape(ROWS_DEV, width)
        aggregate = (summed / degree_dev[:, None].astype(jnp.float32)).astype(jnp.bfloat16)
        mixed = jnp.dot(own_rows, self_weight, preferred_element_type=jnp.float32) + jnp.dot(aggregate, neigh_weight, preferred_element_type=jnp.float32)
        active = jnp.maximum(mixed, 0.0)
        scaled = active * lax.rsqrt(lax.optimization_barrier(jnp.mean(active * active, axis=-1, keepdims=True)) + 1e-06)
        return scaled.astype(jnp.bfloat16)
    return lax.map(per_device, (jnp.arange(count, dtype=jnp.int32), hidden_in, tile_index.reshape(count, BLOCKS_DEV, TILE_SLOTS), tile_live.reshape(count, BLOCKS_DEV), tiles.reshape(count, BLOCKS_DEV, TILE_SLOTS, TILE_SIZE, TILE_SIZE), degree.reshape(count, ROWS_DEV)))

def reference(features, enc_weight, pack_index, place_index, halo_send_one, halo_send_two, tile_index_one, tile_index_two, tile_live_one, tile_live_two, tiles_one, tiles_two, degree, self_weight_one, neigh_weight_one, self_weight_two, neigh_weight_two, head_weight):
    count = N_DOM * N_SHARD
    encoded = jnp.maximum(jnp.dot(features, enc_weight, preferred_element_type=jnp.float32), 0.0).astype(jnp.bfloat16)
    width = encoded.shape[1]
    hashed = encoded.reshape(N_DOM, N_SHARD, ROWS_DEV, width)

    def relay_group(packed):
        block, packing, placing = packed
        outgoing = jax.vmap(lambda table, picks: table[picks.reshape(-1)].reshape(N_SHARD, RELAY_CAP, width))(block, packing)
        arrived = jnp.transpose(outgoing, (1, 0, 2, 3)).reshape(N_SHARD, N_SHARD * RELAY_CAP, width)
        return jax.vmap(lambda table, picks: table[picks])(arrived, placing)
    owned = lax.map(relay_group, (hashed, pack_index, place_index)).reshape(count, ROWS_DEV, width)
    layer_one = sage_layer(owned, halo_send_one, tile_index_one, tile_live_one, tiles_one, degree, self_weight_one, neigh_weight_one)
    layer_two = sage_layer(layer_one, halo_send_two, tile_index_two, tile_live_two, tiles_two, degree, self_weight_two, neigh_weight_two)
    embedding = layer_two.reshape(count * ROWS_DEV, width)
    probability = jax.nn.sigmoid(jnp.dot(embedding, head_weight, preferred_element_type=jnp.float32))
    return (embedding, probability)
```

```python
import functools

import jax
import jax.numpy as jnp
from jax import lax
from jax.experimental import pallas as pl
from jax.experimental.pallas import tpu as pltpu
from jax.sharding import PartitionSpec as P

LANES = 128
STEP = 512
VMEM_LIMIT = 56 << 20
MESH = pl.DeviceIdType.MESH


def across(ref, ids, rows):
    def body(r, carry):
        row = ref[pl.ds(r, 1), :]
        wide = jnp.broadcast_to(row, (LANES, LANES)).T
        lane = lax.broadcasted_iota(jnp.int32, (LANES, LANES), 1)
        ids[pl.ds(pl.multiple_of(r * LANES, LANES), LANES), :] = wide - lane
        return carry

    lax.fori_loop(0, rows // LANES, body, 0)


def one_hot(ids, first, count):
    return jnp.concatenate(
        [
            jnp.where(ids == first + c * LANES, 1.0, 0.0).astype(jnp.bfloat16)
            for c in range(count // LANES)
        ],
        axis=1,
    )


def dot(a, b):
    return jnp.dot(a, b, preferred_element_type=jnp.float32)


def select_rows(ids, table, acc):
    depth = 2 * STEP
    acc[...] = jnp.zeros_like(acc)

    def body(k, carry):
        base = pl.multiple_of(k * depth, depth)
        acc[...] += dot(one_hot(ids, base, depth), table[pl.ds(base, depth), :])
        return carry

    lax.fori_loop(0, table.shape[0] // depth, body, 0)
    return acc[...].astype(jnp.bfloat16)


def flipped(a, b, n):
    total, bit = 0, 1
    while bit < n:
        p, q = (a // bit) % 2, (b // bit) % 2
        total = total + bit * (p + q - 2 * p * q)
        bit *= 2
    return total


def relay_kernel(
    n,
    features,
    weight,
    packing,
    placing,
    sending,
    owned,
    outgoing,
    feats,
    encoded,
    stage,
    recv,
    pack_ids,
    place_ids,
    send_ids,
    acc,
    sel,
    feat_sem,
    send_sem,
    recv_sem,
):
    rows, width = owned.shape
    cap = rows // n
    dom, me = lax.axis_index("dom"), lax.axis_index("shard")
    parts = rows // STEP

    def chunk(c):
        here = pl.ds(pl.multiple_of(c * STEP, STEP), STEP)
        return pltpu.make_async_copy(features.at[here, :], feats.at[here, :], feat_sem.at[c])

    for c in range(parts):
        chunk(c).start()
    barrier = pltpu.get_barrier_semaphore()

    def greet(m, carry):
        pl.semaphore_signal(
            barrier, inc=1, device_id=(dom, flipped(me, m, n)), device_id_type=MESH
        )
        return carry

    lax.fori_loop(1, n, greet, 0)
    across(packing, pack_ids, rows)
    across(placing, place_ids, rows)
    across(sending, send_ids, outgoing.shape[0])

    def encode(c, carry):
        chunk(c).wait()
        here = pl.ds(pl.multiple_of(c * STEP, STEP), STEP)
        encoded[here, :] = jnp.maximum(dot(feats[here, :], weight[...]), 0.0).astype(jnp.bfloat16)
        return carry

    lax.fori_loop(0, parts, encode, 0)
    pl.semaphore_wait(barrier, n - 1)

    def ids_for(t):
        return pack_ids[pl.ds(pl.multiple_of(t * cap, cap), cap), :]

    def transfer(m):
        return pltpu.make_async_remote_copy(
            src_ref=stage.at[m],
            dst_ref=recv.at[m],
            send_sem=send_sem.at[m],
            recv_sem=recv_sem.at[m],
            device_id=(dom, flipped(me, m, n)),
            device_id_type=MESH,
        )

    def pack(step, carry):
        m = n - step
        stage[m] = select_rows(ids_for(flipped(me, m, n)), encoded, acc)
        transfer(m).start()
        return carry

    lax.fori_loop(1, n, pack, 0)
    stage[0] = select_rows(ids_for(me), encoded, acc)

    def place(source, block, fresh):
        def body(r, carry):
            here = pl.ds(pl.multiple_of(r * STEP, STEP), STEP)
            found = dot(one_hot(place_ids[here, :], source * cap, cap), block[...]).astype(
                jnp.bfloat16
            )
            owned[here, :] = found if fresh else owned[here, :] + found
            return carry

        lax.fori_loop(0, parts, body, 0)

    place(me, stage.at[0], True)

    def arrive(step, carry):
        m = n - step
        transfer(m).wait_recv()
        place(flipped(me, m, n), recv.at[m], False)
        return carry

    lax.fori_loop(1, n, arrive, 0)

    def leave(m, carry):
        transfer(m).wait_send()
        return carry

    lax.fori_loop(1, n, leave, 0)

    def boundary(r, carry):
        here = pl.ds(pl.multiple_of(r * STEP, STEP), STEP)
        outgoing[here, :] = select_rows(send_ids[here, :], owned, sel)
        return carry

    lax.fori_loop(0, outgoing.shape[0] // STEP, boundary, 0)


def relay(features, weight, packing, placing, sending, n):
    rows, depth = features.shape
    width = weight.shape[1]
    cap = rows // n
    count = sending.size
    vmem = pl.BlockSpec(memory_space=pltpu.VMEM)
    flops = 2 * rows * width * (depth + 2 * rows + count)
    return pl.pallas_call(
        functools.partial(relay_kernel, n),
        out_shape=(
            jax.ShapeDtypeStruct((rows, width), jnp.bfloat16),
            jax.ShapeDtypeStruct((count, width), jnp.bfloat16),
        ),
        in_specs=[pl.BlockSpec(memory_space=pl.ANY)] + [vmem] * 4,
        out_specs=(vmem, vmem),
        scratch_shapes=[
            pltpu.VMEM((rows, depth), jnp.bfloat16),
            pltpu.VMEM((rows, width), jnp.bfloat16),
            pltpu.VMEM((n, cap, width), jnp.bfloat16),
            pltpu.VMEM((n, cap, width), jnp.bfloat16),
            pltpu.VMEM((rows, LANES), jnp.int32),
            pltpu.VMEM((rows, LANES), jnp.int32),
            pltpu.VMEM((count, LANES), jnp.int32),
            pltpu.VMEM((cap, width), jnp.float32),
            pltpu.VMEM((STEP, width), jnp.float32),
            pltpu.SemaphoreType.DMA((rows // STEP,)),
            pltpu.SemaphoreType.DMA((n,)),
            pltpu.SemaphoreType.DMA((n,)),
        ],
        compiler_params=pltpu.CompilerParams(
            collective_id=0, has_side_effects=True, vmem_limit_bytes=VMEM_LIMIT
        ),
        cost_estimate=pl.CostEstimate(
            flops=flops, bytes_accessed=rows * depth * 2, transcendentals=0
        ),
    )(
        features,
        weight,
        packing.reshape(-1, LANES),
        placing.reshape(-1, LANES),
        sending.reshape(-1, LANES),
    )


def layer_kernel(
    last,
    index,
    live,
    hidden,
    halo,
    tiles,
    degree,
    self_weight,
    neigh_weight,
    extra,
    out,
    second,
    sources,
    aggregate,
    ids,
    sem,
):
    step = pl.program_id(0)
    rows = hidden.shape[0]
    blocks, slots, size = tiles.shape[:3]

    @pl.when(step == 0)
    def _():
        own = pltpu.make_async_copy(hidden, sources.at[pl.ds(0, rows), :], sem.at[0])
        far = pltpu.make_async_copy(halo, sources.at[pl.ds(rows, halo.shape[0]), :], sem.at[1])
        own.start()
        far.start()
        if not last:
            across(extra, ids, ids.shape[0])
        own.wait()
        far.wait()

    for j in range(blocks):
        block = step * blocks + j
        lit = live[block]
        lhs = jnp.concatenate(
            [
                jnp.where(k < lit, tiles[j, k], jnp.zeros((), jnp.bfloat16))
                for k in range(slots)
            ],
            axis=1,
        )
        rhs = jnp.concatenate(
            [
                sources[pl.ds(pl.multiple_of(index[block * slots + k] * size, size), size), :]
                for k in range(slots)
            ],
            axis=0,
        )
        given = degree[pl.ds(block, 1), :].astype(jnp.float32)
        share = 1.0 / jnp.broadcast_to(given, (LANES, LANES)).T
        total = dot(lhs, rhs)
        aggregate[j * size : (j + 1) * size, :] = (
            total * jnp.concatenate([share] * (total.shape[1] // LANES), axis=1)
        ).astype(jnp.bfloat16)
    span = blocks * size
    own_rows = sources[pl.ds(pl.multiple_of(step * span, span), span), :]
    mixed = dot(own_rows, self_weight[...]) + dot(aggregate[...], neigh_weight[...])
    active = jnp.maximum(mixed, 0.0)
    scale = lax.rsqrt(jnp.mean(active * active, axis=-1, keepdims=True) + 1e-06)
    result = (active * scale).astype(jnp.bfloat16)
    out[...] = result
    if last:
        logits = lax.dot_general(
            extra[...], result, (((1,), (1,)), ((), ())), preferred_element_type=jnp.float32
        )
        second[...] = jax.nn.sigmoid(logits[0:1, :])[None]
    else:

        def boundary(r, carry):
            here = pl.ds(pl.multiple_of(r * STEP, STEP), STEP)
            found = dot(one_hot(ids[here, :], step * span, span), result).astype(jnp.bfloat16)
            second[here, :] = jnp.where(step == 0, jnp.zeros_like(found), second[here, :]) + found
            return carry

        lax.fori_loop(0, second.shape[0] // STEP, boundary, 0)


def sage_layer(
    hidden, halo, tile_index, tile_live, tiles, degree, self_weight, neigh_weight, extra, last
):
    rows, width = hidden.shape
    blocks_all, slots, size = tiles.shape[:3]
    per_step = STEP // size
    steps = blocks_all // per_step
    count = halo.shape[0]
    if last:
        extra = jnp.broadcast_to(extra[None, :], (16, width))
        second_shape = jax.ShapeDtypeStruct((steps, 1, STEP), jnp.float32)
        second_spec = pl.BlockSpec((1, 1, STEP), lambda i, *_: (i, 0, 0))
    else:
        extra = extra.reshape(-1, LANES)
        second_shape = jax.ShapeDtypeStruct((extra.size, width), jnp.bfloat16)
        second_spec = pl.BlockSpec((extra.size, width), lambda i, *_: (0, 0))

    def whole(a):
        return pl.BlockSpec(a.shape, lambda i, *_: (0, 0))

    degree = degree.reshape(-1, LANES)
    any_spec = pl.BlockSpec(memory_space=pl.ANY)
    return pl.pallas_call(
        functools.partial(layer_kernel, last),
        out_shape=(jax.ShapeDtypeStruct((rows, width), jnp.bfloat16), second_shape),
        grid_spec=pltpu.PrefetchScalarGridSpec(
            num_scalar_prefetch=2,
            grid=(steps,),
            in_specs=[
                any_spec,
                any_spec,
                pl.BlockSpec((per_step, slots, size, size), lambda i, *_: (i, 0, 0, 0)),
                whole(degree),
                whole(self_weight),
                whole(neigh_weight),
                whole(extra),
            ],
            out_specs=(pl.BlockSpec((STEP, width), lambda i, *_: (i, 0)), second_spec),
            scratch_shapes=[
                pltpu.VMEM((rows + count, width), jnp.bfloat16),
                pltpu.VMEM((STEP, width), jnp.bfloat16),
                pltpu.VMEM((count, LANES), jnp.int32),
                pltpu.SemaphoreType.DMA((2,)),
            ],
        ),
        compiler_params=pltpu.CompilerParams(vmem_limit_bytes=VMEM_LIMIT),
        cost_estimate=pl.CostEstimate(
            flops=2 * rows * width * (slots * size + 2 * width),
            bytes_accessed=tiles.size * 2 + 4 * rows * width,
            transcendentals=0,
        ),
    )(
        tile_index.reshape(-1),
        tile_live,
        hidden,
        halo,
        tiles,
        degree,
        self_weight,
        neigh_weight,
        extra,
    )


def exchange(outgoing, devices):
    width = outgoing.shape[-1]
    return lax.all_to_all(
        outgoing.reshape(devices, -1, width),
        ("dom", "shard"),
        split_axis=0,
        concat_axis=0,
        tiled=True,
    ).reshape(-1, width)


def per_device(
    features,
    enc_weight,
    pack_index,
    place_index,
    halo_send_one,
    halo_send_two,
    tile_index_one,
    tile_index_two,
    tile_live_one,
    tile_live_two,
    tiles_one,
    tiles_two,
    degree,
    self_weight_one,
    neigh_weight_one,
    self_weight_two,
    neigh_weight_two,
    head_weight,
):
    group_size = lax.axis_size("shard")
    devices = lax.axis_size("dom") * group_size
    owned, outgoing = relay(
        features, enc_weight, pack_index, place_index, halo_send_one, group_size
    )
    layer_one, outgoing = sage_layer(
        owned,
        exchange(outgoing, devices),
        tile_index_one,
        tile_live_one,
        tiles_one,
        degree,
        self_weight_one,
        neigh_weight_one,
        halo_send_two,
        False,
    )
    embedding, probability = sage_layer(
        layer_one,
        exchange(outgoing, devices),
        tile_index_two,
        tile_live_two,
        tiles_two,
        degree,
        self_weight_two,
        neigh_weight_two,
        head_weight,
        True,
    )
    return (embedding, probability.reshape(-1))


def solution(mesh):
    placed = (
        P(("dom", "shard"), None),
        P(),
        P("dom", "shard", None, None),
        P("dom", "shard", None),
        P("dom", "shard", None, None, None),
        P("dom", "shard", None, None, None),
        P(("dom", "shard"), None),
        P(("dom", "shard"), None),
        P(("dom", "shard")),
        P(("dom", "shard")),
        P(("dom", "shard"), None, None, None),
        P(("dom", "shard"), None, None, None),
        P(("dom", "shard")),
        P(),
        P(),
        P(),
        P(),
        P(),
    )
    return jax.shard_map(
        per_device,
        mesh=mesh,
        in_specs=placed,
        out_specs=(P(("dom", "shard"), None), P(("dom", "shard"))),
        check_vma=False,
    )
```

```python
import functools

import jax
import jax.numpy as jnp
from jax import lax
from jax.experimental import pallas as pl
from jax.experimental.pallas import tpu as pltpu
from jax.sharding import PartitionSpec as P

LANES = 128
STEP = 512
VMEM_LIMIT = 56 << 20
MESH = pl.DeviceIdType.MESH


def across(ref, ids):
    lines, columns = ref.shape
    lane = lax.broadcasted_iota(jnp.int32, (LANES, LANES), 1)
    for r in range(lines):
        for c in range(columns // LANES):
            row = ref[r : r + 1, c * LANES : (c + 1) * LANES]
            first = r * columns + c * LANES
            ids[first : first + LANES, :] = jnp.broadcast_to(row, (LANES, LANES)).T - lane


def one_hot(ids, first, count):
    return jnp.concatenate(
        [
            jnp.where(ids == first + c * LANES, 1.0, 0.0).astype(jnp.bfloat16)
            for c in range(count // LANES)
        ],
        axis=1,
    )


def dot(a, b):
    return jnp.dot(a, b, preferred_element_type=jnp.float32)


def select_rows(ids, table, acc):
    depth = 2 * STEP
    acc[...] = jnp.zeros_like(acc)

    def body(k, carry):
        base = pl.multiple_of(k * depth, depth)
        acc[...] += dot(one_hot(ids, base, depth), table[pl.ds(base, depth), :])
        return carry

    lax.fori_loop(0, table.shape[0] // depth, body, 0)
    return acc[...].astype(jnp.bfloat16)


def flipped(a, b, n):
    total, bit = 0, 1
    while bit < n:
        p, q = (a // bit) % 2, (b // bit) % 2
        total = total + bit * (p + q - 2 * p * q)
        bit *= 2
    return total


def relay_kernel(
    n,
    features,
    weight,
    packing,
    placing,
    sending,
    owned,
    outgoing,
    feats,
    encoded,
    stage,
    recv,
    pack_ids,
    place_ids,
    send_ids,
    acc,
    sel,
    feat_sem,
    send_sem,
    recv_sem,
):
    rows, width = owned.shape
    cap = rows // n
    dom, me = lax.axis_index("dom"), lax.axis_index("shard")
    parts = rows // STEP

    def chunk(c):
        here = pl.ds(pl.multiple_of(c * STEP, STEP), STEP)
        return pltpu.make_async_copy(features.at[here, :], feats.at[here, :], feat_sem.at[c])

    for c in range(parts):
        chunk(c).start()
    barrier = pltpu.get_barrier_semaphore()

    def greet(m, carry):
        pl.semaphore_signal(
            barrier, inc=1, device_id=(dom, flipped(me, m, n)), device_id_type=MESH
        )
        return carry

    lax.fori_loop(1, n, greet, 0)
    across(packing, pack_ids)
    across(placing, place_ids)
    across(sending, send_ids)

    def encode(c, carry):
        chunk(c).wait()
        here = pl.ds(pl.multiple_of(c * STEP, STEP), STEP)
        encoded[here, :] = jnp.maximum(dot(feats[here, :], weight[...]), 0.0).astype(jnp.bfloat16)
        return carry

    lax.fori_loop(0, parts, encode, 0)
    pl.semaphore_wait(barrier, n - 1)

    def ids_for(t):
        return pack_ids[pl.ds(pl.multiple_of(t * cap, cap), cap), :]

    def transfer(m):
        return pltpu.make_async_remote_copy(
            src_ref=stage.at[m],
            dst_ref=recv.at[m],
            send_sem=send_sem.at[m],
            recv_sem=recv_sem.at[m],
            device_id=(dom, flipped(me, m, n)),
            device_id_type=MESH,
        )

    def pack(step, carry):
        m = n - step
        stage[m] = select_rows(ids_for(flipped(me, m, n)), encoded, acc)
        transfer(m).start()
        return carry

    lax.fori_loop(1, n, pack, 0)
    stage[0] = select_rows(ids_for(me), encoded, acc)

    def place(source, block, fresh):
        def body(r, carry):
            here = pl.ds(pl.multiple_of(r * STEP, STEP), STEP)
            found = dot(one_hot(place_ids[here, :], source * cap, cap), block[...]).astype(
                jnp.bfloat16
            )
            owned[here, :] = found if fresh else owned[here, :] + found
            return carry

        lax.fori_loop(0, parts, body, 0)

    place(me, stage.at[0], True)

    def arrive(step, carry):
        m = n - step
        transfer(m).wait_recv()
        place(flipped(me, m, n), recv.at[m], False)
        return carry

    lax.fori_loop(1, n, arrive, 0)

    def leave(m, carry):
        transfer(m).wait_send()
        return carry

    lax.fori_loop(1, n, leave, 0)

    def boundary(r, carry):
        here = pl.ds(pl.multiple_of(r * STEP, STEP), STEP)
        outgoing[here, :] = select_rows(send_ids[here, :], owned, sel)
        return carry

    lax.fori_loop(0, outgoing.shape[0] // STEP, boundary, 0)


def relay(features, weight, packing, placing, sending, n):
    rows, depth = features.shape
    width = weight.shape[1]
    cap = rows // n
    count = sending.size
    vmem = pl.BlockSpec(memory_space=pltpu.VMEM)
    flops = 2 * rows * width * (depth + 2 * rows + count)
    return pl.pallas_call(
        functools.partial(relay_kernel, n),
        out_shape=(
            jax.ShapeDtypeStruct((rows, width), jnp.bfloat16),
            jax.ShapeDtypeStruct((count, width), jnp.bfloat16),
        ),
        in_specs=[pl.BlockSpec(memory_space=pl.ANY)] + [vmem] * 4,
        out_specs=(vmem, vmem),
        scratch_shapes=[
            pltpu.VMEM((rows, depth), jnp.bfloat16),
            pltpu.VMEM((rows, width), jnp.bfloat16),
            pltpu.VMEM((n, cap, width), jnp.bfloat16),
            pltpu.VMEM((n, cap, width), jnp.bfloat16),
            pltpu.VMEM((rows, LANES), jnp.int32),
            pltpu.VMEM((rows, LANES), jnp.int32),
            pltpu.VMEM((count, LANES), jnp.int32),
            pltpu.VMEM((cap, width), jnp.float32),
            pltpu.VMEM((STEP, width), jnp.float32),
            pltpu.SemaphoreType.DMA((rows // STEP,)),
            pltpu.SemaphoreType.DMA((n,)),
            pltpu.SemaphoreType.DMA((n,)),
        ],
        compiler_params=pltpu.CompilerParams(
            collective_id=0, has_side_effects=True, vmem_limit_bytes=VMEM_LIMIT
        ),
        cost_estimate=pl.CostEstimate(
            flops=flops, bytes_accessed=rows * depth * 2, transcendentals=0
        ),
    )(
        features,
        weight,
        packing.reshape(n, cap),
        placing.reshape(1, -1),
        sending.reshape(-1, LANES),
    )


def layer_kernel(
    last,
    groups,
    n,
    near,
    far,
    hidden,
    outgoing,
    tiles,
    degree,
    self_weight,
    neigh_weight,
    extra,
    out,
    second,
    sources,
    halo,
    far_tiles,
    near_sum,
    self_part,
    ids,
    sem,
    send_sem,
    recv_sem,
):
    step = pl.program_id(0)
    count = outgoing.shape[0]
    blocks, slots, size = tiles.shape[:3]
    span = blocks * size
    own_blocks = hidden.shape[0]
    steps = own_blocks // blocks
    far_blocks = count // size
    devices = groups * n
    bound = count // devices
    me = lax.axis_index("dom") * n + lax.axis_index("shard")

    def device(e):
        return (e // n, e % n)

    def rows_of(e):
        return pl.ds(pl.multiple_of(e * bound, bound), bound)

    def transfer(q):
        to = (me + q) % devices
        return pltpu.make_async_remote_copy(
            src_ref=outgoing.at[rows_of(to), :],
            dst_ref=halo.at[rows_of(me), :],
            send_sem=send_sem.at[q],
            recv_sem=recv_sem.at[q],
            device_id=device(to),
            device_id_type=MESH,
        )

    def own_copies():
        return [
            pltpu.make_async_copy(hidden, sources.at[pl.ds(0, own_blocks)], sem.at[0]),
            pltpu.make_async_copy(
                outgoing.at[rows_of(me), :], halo.at[rows_of(me), :], sem.at[1]
            ),
        ]

    @pl.when(step == 0)
    def _():
        for copy in own_copies():
            copy.start()
        barrier = pltpu.get_barrier_semaphore()

        def greet(q, carry):
            pl.semaphore_signal(
                barrier, inc=1, device_id=device((me + q) % devices), device_id_type=MESH
            )
            return carry

        lax.fori_loop(1, devices, greet, 0)
        sources[own_blocks] = jnp.zeros_like(sources[own_blocks])
        if not last:
            across(extra, ids)
        pl.semaphore_wait(barrier, devices - 1)

        def send(q, carry):
            transfer(q).start()
            return carry

        lax.fori_loop(1, devices, send, 0)
        for copy in own_copies():
            copy.wait()

    @pl.when(step < steps)
    def _():
        for j in range(blocks):
            block = step * blocks + j
            first = pl.multiple_of(block * size, size)
            lhs = jnp.concatenate([tiles[j, k] for k in range(slots)], axis=1)
            rhs = jnp.concatenate(
                [sources[near[block * slots + k]] for k in range(slots)], axis=0
            )
            near_sum[pl.ds(first, size), :] = dot(lhs, rhs)
            for f in range(count // size):
                total = None
                for k in range(slots):
                    flag = jnp.full((size, size), far[(block * slots + k) * far_blocks + f])
                    term = tiles[j, k] * flag.astype(jnp.bfloat16)
                    total = term if total is None else total + term
                far_tiles[pl.ds(first, size), f * size : (f + 1) * size] = total
        here = pl.ds(pl.multiple_of(step * span, span), span)
        own_rows = sources[pl.ds(step * blocks, blocks)].reshape(span, hidden.shape[2])
        self_part[here, :] = dot(own_rows, self_weight[...])

    @pl.when(step == steps)
    def _():
        def arrive(q, carry):
            transfer(q).wait_recv()
            return carry

        lax.fori_loop(1, devices, arrive, 0)

        def leave(q, carry):
            transfer(q).wait_send()
            return carry

        lax.fori_loop(1, devices, leave, 0)

    @pl.when(step >= steps)
    def _():
        turn = step - steps
        here = pl.ds(pl.multiple_of(turn * span, span), span)
        width = out.shape[1]
        shares = []
        for j in range(blocks):
            given = degree[pl.ds(turn * blocks + j, 1), :].astype(jnp.float32)
            shares.append(1.0 / jnp.broadcast_to(given, (LANES, LANES)).T)
        share = jnp.concatenate(shares, axis=0)
        total = near_sum[here, :] + dot(far_tiles[here, :], halo[...])
        aggregate = (total * jnp.concatenate([share] * (width // LANES), axis=1)).astype(
            jnp.bfloat16
        )
        mixed = self_part[here, :] + dot(aggregate, neigh_weight[...])
        active = jnp.maximum(mixed, 0.0)
        scale = lax.rsqrt(jnp.mean(active * active, axis=-1, keepdims=True) + 1e-06)
        result = (active * scale).astype(jnp.bfloat16)
        out[...] = result
        if last:
            logits = lax.dot_general(
                extra[...], result, (((1,), (1,)), ((), ())), preferred_element_type=jnp.float32
            )
            second[...] = jax.nn.sigmoid(logits[0:1, :])[None]
        else:

            @pl.when(turn == 0)
            def _():
                second[...] = jnp.zeros_like(second)

            def boundary(r, carry):
                part = pl.ds(pl.multiple_of(r * STEP, STEP), STEP)
                found = dot(one_hot(ids[part, :], turn * span, span), result)
                second[part, :] = second[part, :] + found.astype(jnp.bfloat16)
                return carry

            lax.fori_loop(0, second.shape[0] // STEP, boundary, 0)


def sage_layer(
    hidden, outgoing, tile_index, tile_live, tiles, degree, self_weight, neigh_weight, extra, last
):
    groups, n = lax.axis_size("dom"), lax.axis_size("shard")
    rows, width = hidden.shape
    blocks_all, slots, size = tiles.shape[:3]
    per_step = STEP // size
    steps = blocks_all // per_step
    count = outgoing.shape[0]

    used = jnp.where(
        jnp.arange(slots, dtype=jnp.int32)[None, :] < tile_live[:, None], tile_index, -1
    )
    near = jnp.where((used >= 0) & (used < blocks_all), used, blocks_all)
    far_block = blocks_all + jnp.arange(count // size, dtype=jnp.int32)
    far = (used[:, :, None] == far_block).astype(jnp.float32)

    def late(i):
        return (i // steps) * (i - steps)

    if last:
        extra = jnp.broadcast_to(extra[None, :], (16, width))
        second_shape = jax.ShapeDtypeStruct((steps, 1, STEP), jnp.float32)
        second_spec = pl.BlockSpec((1, 1, STEP), lambda i, *_: (late(i), 0, 0))
    else:
        extra = extra.reshape(-1, LANES)
        second_shape = jax.ShapeDtypeStruct((extra.size, width), jnp.bfloat16)
        second_spec = pl.BlockSpec((extra.size, width), lambda i, *_: (0, 0))

    def whole(a):
        return pl.BlockSpec(a.shape, lambda i, *_: (0, 0))

    degree = degree.reshape(-1, LANES)
    any_spec = pl.BlockSpec(memory_space=pl.ANY)
    return pl.pallas_call(
        functools.partial(layer_kernel, last, groups, n),
        out_shape=(jax.ShapeDtypeStruct((rows, width), jnp.bfloat16), second_shape),
        grid_spec=pltpu.PrefetchScalarGridSpec(
            num_scalar_prefetch=2,
            grid=(2 * steps,),
            in_specs=[
                any_spec,
                any_spec,
                pl.BlockSpec(
                    (per_step, slots, size, size),
                    lambda i, *_: (i - (i // steps) * (i - steps + 1), 0, 0, 0),
                ),
                whole(degree),
                whole(self_weight),
                whole(neigh_weight),
                whole(extra),
            ],
            out_specs=(pl.BlockSpec((STEP, width), lambda i, *_: (late(i), 0)), second_spec),
            scratch_shapes=[
                pltpu.VMEM((blocks_all + 1, size, width), jnp.bfloat16),
                pltpu.VMEM((count, width), jnp.bfloat16),
                pltpu.VMEM((rows, count), jnp.bfloat16),
                pltpu.VMEM((rows, width), jnp.float32),
                pltpu.VMEM((rows, width), jnp.float32),
                pltpu.VMEM((count, LANES), jnp.int32),
                pltpu.SemaphoreType.DMA((2,)),
                pltpu.SemaphoreType.DMA((groups * n,)),
                pltpu.SemaphoreType.DMA((groups * n,)),
            ],
        ),
        compiler_params=pltpu.CompilerParams(
            collective_id=2 if last else 1, has_side_effects=True, vmem_limit_bytes=VMEM_LIMIT
        ),
        cost_estimate=pl.CostEstimate(
            flops=2 * rows * width * (slots * size + 2 * width),
            bytes_accessed=tiles.size * 2 + 4 * rows * width,
            transcendentals=0,
        ),
    )(
        near.reshape(-1),
        far.reshape(-1),
        hidden.reshape(blocks_all, size, width),
        outgoing,
        tiles,
        degree,
        self_weight,
        neigh_weight,
        extra,
    )


def per_device(
    features,
    enc_weight,
    pack_index,
    place_index,
    halo_send_one,
    halo_send_two,
    tile_index_one,
    tile_index_two,
    tile_live_one,
    tile_live_two,
    tiles_one,
    tiles_two,
    degree,
    self_weight_one,
    neigh_weight_one,
    self_weight_two,
    neigh_weight_two,
    head_weight,
):
    group_size = lax.axis_size("shard")
    owned, outgoing = relay(
        features, enc_weight, pack_index, place_index, halo_send_one, group_size
    )
    layer_one, outgoing = sage_layer(
        owned,
        outgoing,
        tile_index_one,
        tile_live_one,
        tiles_one,
        degree,
        self_weight_one,
        neigh_weight_one,
        halo_send_two,
        False,
    )
    embedding, probability = sage_layer(
        layer_one,
        outgoing,
        tile_index_two,
        tile_live_two,
        tiles_two,
        degree,
        self_weight_two,
        neigh_weight_two,
        head_weight,
        True,
    )
    return (embedding, probability.reshape(-1))


def solution(mesh):
    placed = (
        P(("dom", "shard"), None),
        P(),
        P("dom", "shard", None, None),
        P("dom", "shard", None),
        P("dom", "shard", None, None, None),
        P("dom", "shard", None, None, None),
        P(("dom", "shard"), None),
        P(("dom", "shard"), None),
        P(("dom", "shard")),
        P(("dom", "shard")),
        P(("dom", "shard"), None, None, None),
        P(("dom", "shard"), None, None, None),
        P(("dom", "shard")),
        P(),
        P(),
        P(),
        P(),
        P(),
    )
    return jax.shard_map(
        per_device,
        mesh=mesh,
        in_specs=placed,
        out_specs=(P(("dom", "shard"), None), P(("dom", "shard"))),
        check_vma=False,
    )
```

```python
import functools

import jax
import jax.numpy as jnp
from jax import lax
from jax.experimental import pallas as pl
from jax.experimental.pallas import tpu as pltpu
from jax.sharding import PartitionSpec as P

LANES = 128
STEP = 512
VMEM_LIMIT = 56 << 20
MESH = pl.DeviceIdType.MESH


def across(ref, ids):
    lines, columns = ref.shape
    lane = lax.broadcasted_iota(jnp.int32, (LANES, LANES), 1)
    for r in range(lines):
        for c in range(columns // LANES):
            row = ref[r : r + 1, c * LANES : (c + 1) * LANES]
            first = r * columns + c * LANES
            ids[first : first + LANES, :] = jnp.broadcast_to(row, (LANES, LANES)).T - lane


def one_hot(ids, first, count):
    return jnp.concatenate(
        [
            jnp.where(ids == first + c * LANES, 1.0, 0.0).astype(jnp.bfloat16)
            for c in range(count // LANES)
        ],
        axis=1,
    )


def dot(a, b):
    return jnp.dot(a, b, preferred_element_type=jnp.float32)


def select_rows(ids, table, acc):
    depth = 4 * STEP
    acc[...] = jnp.zeros_like(acc)

    def body(k, carry):
        base = pl.multiple_of(k * depth, depth)
        acc[...] += dot(one_hot(ids, base, depth), table[pl.ds(base, depth), :])
        return carry

    lax.fori_loop(0, table.shape[0] // depth, body, 0)
    return acc[...].astype(jnp.bfloat16)


def flipped(a, b, n):
    total, bit = 0, 1
    while bit < n:
        p, q = (a // bit) % 2, (b // bit) % 2
        total = total + bit * (p + q - 2 * p * q)
        bit *= 2
    return total


def relay_kernel(
    n,
    features,
    weight,
    packing,
    placing,
    sending,
    owned,
    outgoing,
    feats,
    encoded,
    stage,
    recv,
    pack_ids,
    place_ids,
    send_ids,
    acc,
    sel,
    feat_sem,
    send_sem,
    recv_sem,
):
    rows, width = owned.shape
    cap = rows // n
    dom, me = lax.axis_index("dom"), lax.axis_index("shard")
    parts = rows // STEP

    def chunk(c):
        here = pl.ds(pl.multiple_of(c * STEP, STEP), STEP)
        return pltpu.make_async_copy(features.at[here, :], feats.at[here, :], feat_sem.at[c])

    for c in range(parts):
        chunk(c).start()
    barrier = pltpu.get_barrier_semaphore()

    def greet(m, carry):
        pl.semaphore_signal(
            barrier, inc=1, device_id=(dom, flipped(me, m, n)), device_id_type=MESH
        )
        return carry

    lax.fori_loop(1, n, greet, 0)
    across(packing, pack_ids)
    across(placing, place_ids)
    across(sending, send_ids)

    def encode(c, carry):
        chunk(c).wait()
        here = pl.ds(pl.multiple_of(c * STEP, STEP), STEP)
        encoded[here, :] = jnp.maximum(dot(feats[here, :], weight[...]), 0.0).astype(jnp.bfloat16)
        return carry

    lax.fori_loop(0, parts, encode, 0)
    pl.semaphore_wait(barrier, n - 1)

    def ids_for(t):
        return pack_ids[pl.ds(pl.multiple_of(t * cap, cap), cap), :]

    def transfer(m):
        return pltpu.make_async_remote_copy(
            src_ref=stage.at[m],
            dst_ref=recv.at[m],
            send_sem=send_sem.at[m],
            recv_sem=recv_sem.at[m],
            device_id=(dom, flipped(me, m, n)),
            device_id_type=MESH,
        )

    def pack(step, carry):
        m = n - step
        stage[m] = select_rows(ids_for(flipped(me, m, n)), encoded, acc)
        transfer(m).start()
        return carry

    lax.fori_loop(1, n, pack, 0)
    stage[0] = select_rows(ids_for(me), encoded, acc)

    def place(source, block, fresh):
        tall = 2 * STEP

        def body(r, carry):
            here = pl.ds(pl.multiple_of(r * tall, tall), tall)
            found = dot(one_hot(place_ids[here, :], source * cap, cap), block[...]).astype(
                jnp.bfloat16
            )
            owned[here, :] = found if fresh else owned[here, :] + found
            return carry

        lax.fori_loop(0, rows // tall, body, 0)

    place(me, stage.at[0], True)

    def arrive(step, carry):
        m = n - step
        transfer(m).wait_recv()
        place(flipped(me, m, n), recv.at[m], False)
        return carry

    lax.fori_loop(1, n, arrive, 0)

    def leave(m, carry):
        transfer(m).wait_send()
        return carry

    lax.fori_loop(1, n, leave, 0)

    def boundary(r, carry):
        here = pl.ds(pl.multiple_of(r * STEP, STEP), STEP)
        outgoing[here, :] = select_rows(send_ids[here, :], owned, sel)
        return carry

    lax.fori_loop(0, outgoing.shape[0] // STEP, boundary, 0)


def relay(features, weight, packing, placing, sending, n):
    rows, depth = features.shape
    width = weight.shape[1]
    cap = rows // n
    count = sending.size
    vmem = pl.BlockSpec(memory_space=pltpu.VMEM)
    flops = 2 * rows * width * (depth + 2 * rows + count)
    return pl.pallas_call(
        functools.partial(relay_kernel, n),
        out_shape=(
            jax.ShapeDtypeStruct((rows, width), jnp.bfloat16),
            jax.ShapeDtypeStruct((count, width), jnp.bfloat16),
        ),
        in_specs=[pl.BlockSpec(memory_space=pl.ANY)] + [vmem] * 4,
        out_specs=(vmem, vmem),
        scratch_shapes=[
            pltpu.VMEM((rows, depth), jnp.bfloat16),
            pltpu.VMEM((rows, width), jnp.bfloat16),
            pltpu.VMEM((n, cap, width), jnp.bfloat16),
            pltpu.VMEM((n, cap, width), jnp.bfloat16),
            pltpu.VMEM((rows, LANES), jnp.int32),
            pltpu.VMEM((rows, LANES), jnp.int32),
            pltpu.VMEM((count, LANES), jnp.int32),
            pltpu.VMEM((cap, width), jnp.float32),
            pltpu.VMEM((STEP, width), jnp.float32),
            pltpu.SemaphoreType.DMA((rows // STEP,)),
            pltpu.SemaphoreType.DMA((n,)),
            pltpu.SemaphoreType.DMA((n,)),
        ],
        compiler_params=pltpu.CompilerParams(
            collective_id=0, has_side_effects=True, vmem_limit_bytes=VMEM_LIMIT
        ),
        cost_estimate=pl.CostEstimate(
            flops=flops, bytes_accessed=rows * depth * 2, transcendentals=0
        ),
    )(
        features,
        weight,
        packing.reshape(n, cap),
        placing.reshape(1, -1),
        sending.reshape(-1, LANES),
    )


def layer_kernel(
    last,
    groups,
    n,
    plan,
    hidden,
    outgoing,
    tiles,
    degree,
    self_weight,
    neigh_weight,
    extra,
    out,
    second,
    sources,
    halo,
    far_tiles,
    near_sum,
    self_part,
    ids,
    sem,
    send_sem,
    recv_sem,
):
    step = pl.program_id(0)
    count = outgoing.shape[0]
    blocks, slots, size = tiles.shape[:3]
    span = blocks * size
    own_blocks = hidden.shape[0]
    steps = own_blocks // blocks
    far_blocks = count // size
    entry = 1 + far_blocks
    start = own_blocks * slots * entry if last else 0
    devices = groups * n
    bound = count // devices
    me = lax.axis_index("dom") * n + lax.axis_index("shard")

    def device(e):
        return (e // n, e % n)

    def rows_of(e):
        return pl.ds(pl.multiple_of(e * bound, bound), bound)

    def transfer(q):
        to = (me + q) % devices
        return pltpu.make_async_remote_copy(
            src_ref=outgoing.at[rows_of(to), :],
            dst_ref=halo.at[rows_of(me), :],
            send_sem=send_sem.at[q],
            recv_sem=recv_sem.at[q],
            device_id=device(to),
            device_id_type=MESH,
        )

    def own_copies():
        return [
            pltpu.make_async_copy(hidden, sources.at[pl.ds(0, own_blocks)], sem.at[0]),
            pltpu.make_async_copy(
                outgoing.at[rows_of(me), :], halo.at[rows_of(me), :], sem.at[1]
            ),
        ]

    @pl.when(step == 0)
    def _():
        for copy in own_copies():
            copy.start()
        barrier = pltpu.get_barrier_semaphore()

        def greet(q, carry):
            pl.semaphore_signal(
                barrier, inc=1, device_id=device((me + q) % devices), device_id_type=MESH
            )
            return carry

        lax.fori_loop(1, devices, greet, 0)
        sources[own_blocks] = jnp.zeros_like(sources[own_blocks])
        if not last:
            across(extra, ids)
        pl.semaphore_wait(barrier, devices - 1)

        def send(q, carry):
            transfer(q).start()
            return carry

        lax.fori_loop(1, devices, send, 0)
        for copy in own_copies():
            copy.wait()

    @pl.when(step < steps)
    def _():
        for j in range(blocks):
            block = step * blocks + j
            first = pl.multiple_of(block * size, size)
            lhs = jnp.concatenate([tiles[j, k] for k in range(slots)], axis=1)
            rhs = jnp.concatenate(
                [sources[plan[start + (block * slots + k) * entry]] for k in range(slots)], axis=0
            )
            near_sum[pl.ds(first, size), :] = dot(lhs, rhs)
            for f in range(count // size):
                total = None
                for k in range(slots):
                    flag = plan[start + (block * slots + k) * entry + 1 + f].astype(jnp.float32)
                    term = tiles[j, k] * jnp.full((size, size), flag).astype(jnp.bfloat16)
                    total = term if total is None else total + term
                far_tiles[pl.ds(first, size), f * size : (f + 1) * size] = total
        here = pl.ds(pl.multiple_of(step * span, span), span)
        own_rows = sources[pl.ds(step * blocks, blocks)].reshape(span, hidden.shape[2])
        self_part[here, :] = dot(own_rows, self_weight[...])

    @pl.when(step == steps)
    def _():
        def arrive(q, carry):
            transfer(q).wait_recv()
            return carry

        lax.fori_loop(1, devices, arrive, 0)

        def leave(q, carry):
            transfer(q).wait_send()
            return carry

        lax.fori_loop(1, devices, leave, 0)

    @pl.when(step >= steps)
    def _():
        turn = step - steps
        here = pl.ds(pl.multiple_of(turn * span, span), span)
        width = out.shape[1]
        shares = []
        for j in range(blocks):
            given = degree[pl.ds(turn * blocks + j, 1), :].astype(jnp.float32)
            shares.append(1.0 / jnp.broadcast_to(given, (LANES, LANES)).T)
        share = jnp.concatenate(shares, axis=0)
        total = near_sum[here, :] + dot(far_tiles[here, :], halo[...])
        aggregate = (total * jnp.concatenate([share] * (width // LANES), axis=1)).astype(
            jnp.bfloat16
        )
        mixed = self_part[here, :] + dot(aggregate, neigh_weight[...])
        active = jnp.maximum(mixed, 0.0)
        scale = lax.rsqrt(jnp.mean(active * active, axis=-1, keepdims=True) + 1e-06)
        result = (active * scale).astype(jnp.bfloat16)
        out[...] = result
        if last:
            logits = lax.dot_general(
                extra[...], result, (((1,), (1,)), ((), ())), preferred_element_type=jnp.float32
            )
            second[...] = jax.nn.sigmoid(logits[0:1, :])[None]
        else:

            @pl.when(turn == 0)
            def _():
                second[...] = jnp.zeros_like(second)

            def boundary(r, carry):
                part = pl.ds(pl.multiple_of(r * STEP, STEP), STEP)
                found = dot(one_hot(ids[part, :], turn * span, span), result)
                second[part, :] = second[part, :] + found.astype(jnp.bfloat16)
                return carry

            lax.fori_loop(0, second.shape[0] // STEP, boundary, 0)


def sage_layer(
    hidden, outgoing, plan, tiles, degree, self_weight, neigh_weight, extra, last
):
    groups, n = lax.axis_size("dom"), lax.axis_size("shard")
    rows, width = hidden.shape
    blocks_all, slots, size = tiles.shape[:3]
    per_step = STEP // size
    steps = blocks_all // per_step
    count = outgoing.shape[0]

    def late(i):
        return (i // steps) * (i - steps)

    if last:
        extra = jnp.broadcast_to(extra[None, :], (16, width))
        second_shape = jax.ShapeDtypeStruct((steps, 1, STEP), jnp.float32)
        second_spec = pl.BlockSpec((1, 1, STEP), lambda i, *_: (late(i), 0, 0))
    else:
        extra = extra.reshape(-1, LANES)
        second_shape = jax.ShapeDtypeStruct((extra.size, width), jnp.bfloat16)
        second_spec = pl.BlockSpec((extra.size, width), lambda i, *_: (0, 0))

    def whole(a):
        return pl.BlockSpec(a.shape, lambda i, *_: (0, 0))

    degree = degree.reshape(-1, LANES)
    any_spec = pl.BlockSpec(memory_space=pl.ANY)
    return pl.pallas_call(
        functools.partial(layer_kernel, last, groups, n),
        out_shape=(jax.ShapeDtypeStruct((rows, width), jnp.bfloat16), second_shape),
        grid_spec=pltpu.PrefetchScalarGridSpec(
            num_scalar_prefetch=1,
            grid=(2 * steps,),
            in_specs=[
                any_spec,
                any_spec,
                pl.BlockSpec(
                    (per_step, slots, size, size),
                    lambda i, *_: (i - (i // steps) * (i - steps + 1), 0, 0, 0),
                ),
                whole(degree),
                whole(self_weight),
                whole(neigh_weight),
                whole(extra),
            ],
            out_specs=(pl.BlockSpec((STEP, width), lambda i, *_: (late(i), 0)), second_spec),
            scratch_shapes=[
                pltpu.VMEM((blocks_all + 1, size, width), jnp.bfloat16),
                pltpu.VMEM((count, width), jnp.bfloat16),
                pltpu.VMEM((rows, count), jnp.bfloat16),
                pltpu.VMEM((rows, width), jnp.float32),
                pltpu.VMEM((rows, width), jnp.float32),
                pltpu.VMEM((count, LANES), jnp.int32),
                pltpu.SemaphoreType.DMA((2,)),
                pltpu.SemaphoreType.DMA((groups * n,)),
                pltpu.SemaphoreType.DMA((groups * n,)),
            ],
        ),
        compiler_params=pltpu.CompilerParams(
            collective_id=2 if last else 1, has_side_effects=True, vmem_limit_bytes=VMEM_LIMIT
        ),
        cost_estimate=pl.CostEstimate(
            flops=2 * rows * width * (slots * size + 2 * width),
            bytes_accessed=tiles.size * 2 + 4 * rows * width,
            transcendentals=0,
        ),
    )(
        plan,
        hidden.reshape(blocks_all, size, width),
        outgoing,
        tiles,
        degree,
        self_weight,
        neigh_weight,
        extra,
    )


def slot_plan(tile_index, tile_live, far_count):
    blocks, slots = tile_index.shape[1:]
    on = jnp.arange(slots, dtype=jnp.int32)[None, None, :] < tile_live[:, :, None]
    used = jnp.where(on, tile_index, -1)[..., None]
    near = jnp.where((used >= 0) & (used < blocks), used, blocks)
    part = jnp.arange(1 + far_count, dtype=jnp.int32)
    flags = (used == blocks - 1 + part).astype(jnp.int32)
    return jnp.where(part == 0, near, flags).reshape(-1)


def per_device(
    features,
    enc_weight,
    pack_index,
    place_index,
    halo_send_one,
    halo_send_two,
    tile_index_one,
    tile_index_two,
    tile_live_one,
    tile_live_two,
    tiles_one,
    tiles_two,
    degree,
    self_weight_one,
    neigh_weight_one,
    self_weight_two,
    neigh_weight_two,
    head_weight,
):
    group_size = lax.axis_size("shard")
    plan = slot_plan(
        jnp.stack([tile_index_one, tile_index_two]),
        jnp.stack([tile_live_one, tile_live_two]),
        halo_send_one.size // tiles_one.shape[2],
    )
    owned, outgoing = relay(
        features, enc_weight, pack_index, place_index, halo_send_one, group_size
    )
    layer_one, outgoing = sage_layer(
        owned,
        outgoing,
        plan,
        tiles_one,
        degree,
        self_weight_one,
        neigh_weight_one,
        halo_send_two,
        False,
    )
    embedding, probability = sage_layer(
        layer_one,
        outgoing,
        plan,
        tiles_two,
        degree,
        self_weight_two,
        neigh_weight_two,
        head_weight,
        True,
    )
    return (embedding, probability.reshape(-1))


def solution(mesh):
    placed = (
        P(("dom", "shard"), None),
        P(),
        P("dom", "shard", None, None),
        P("dom", "shard", None),
        P("dom", "shard", None, None, None),
        P("dom", "shard", None, None, None),
        P(("dom", "shard"), None),
        P(("dom", "shard"), None),
        P(("dom", "shard")),
        P(("dom", "shard")),
        P(("dom", "shard"), None, None, None),
        P(("dom", "shard"), None, None, None),
        P(("dom", "shard")),
        P(),
        P(),
        P(),
        P(),
        P(),
    )
    return jax.shard_map(
        per_device,
        mesh=mesh,
        in_specs=placed,
        out_specs=(P(("dom", "shard"), None), P(("dom", "shard"))),
        check_vma=False,
    )
```
